32 devices in a mesh: shard: 16 (over z, y, core), rep: 2 (over x).
Axes of the slice: x: 2, y: 2, z: 4, core: 2. Of those that a mesh axis runs over, the one named last changes fastest.
Arguments:
- images_in: bfloat16 [256, 196, 512], P(('shard', 'rep')), may hold values from -6 to 6
- norm_gains: bfloat16 [2, 2, 512], P(None, None, 'shard'), may hold values from 0.25 to 1.75
- norm_biases: bfloat16 [2, 2, 512], P(None, None, 'shard'), may hold values from -3 to 3
- qkv_weight: bfloat16 [2, 512, 1536], P(None, 'shard'), may hold values from -0.375 to 0.375
- proj_weight: bfloat16 [2, 512, 512], P(None, 'shard'), may hold values from -0.75 to 0.75
- up_weight: bfloat16 [2, 512, 2048], P(None, 'shard'), may hold values from -0.25 to 0.25
- up_bias: bfloat16 [2, 2048], P(None, 'shard'), may hold values from -3 to 3
- down_weight: bfloat16 [2, 2048, 512], P(None, 'shard'), may hold values from -0.25 to 0.25
- rel_table: float32 [2, 169, 16], replicated, may hold values from -3 to 3
- image_counts: int32 [32], P(('shard', 'rep')), may hold values from 1 to 8, as said below
- cotangent: bfloat16 [256, 196, 512], P(('shard', 'rep')), may hold values from -6 to 6
Outputs:
- block_out: float32 [256, 196, 512], P(('shard', 'rep'))
- grad_images: float32 [256, 196, 512], P(('shard', 'rep'))
- grad_gains: float32 [2, 2, 512], P(None, None, 'shard')
- grad_biases: float32 [2, 2, 512], P(None, None, 'shard')
- grad_qkv: float32 [2, 512, 1536], P(None, 'shard')
- grad_proj: float32 [2, 512, 512], P(None, 'shard')
- grad_up: float32 [2, 512, 2048], P(None, 'shard')
- grad_up_bias: float32 [2, 2048], P(None, 'shard')
- grad_down: float32 [2, 2048, 512], P(None, 'shard')
- grad_table: float32 [2, 169, 16], replicated
The draws below stay inside these ranges and needn't reach their ends.
Inputs may be any that keep to these rules, and one draw needn't show every extreme that they name: Device d (in the order of shard, then rep) holds images in its first image_counts[d] of its 8 slots; the other slots are padding whose cotangent does not count. Some device has all 8 slots filled.
All inputs are finite; a program needn't handle non-finite values.
Results may differ from the reference program's by a relative error of at most 0.025.
Values may be sent and summed in bfloat16 or wider, within the bound.
No kernel may reach another device: no remote copies, remote signals or barrier semaphores. Data moves between devices by JAX's collectives and lax.ppermute only.
A program may use at most 320 MiB of HBM per device.

```python
import jax
import jax.numpy as jnp
from jax import lax

HEADS = 16
FF = 2048
D = 512
WIN = 7
SIDE = 14
SHIFT = 3
REL = 169
LAYERS = 2
IMG_DEV = 8
IMAGES = 256
N_SHARD = 16
N_REP = 2


def draw_image_counts(key, part):
    device_total = N_SHARD * N_REP
    counts = jax.random.randint(jax.random.fold_in(key, 11), (device_total,), 1, IMG_DEV + 1)
    position = jax.random.randint(jax.random.fold_in(key, 12), (), 0, device_total)
    counts = jnp.where(jnp.arange(device_total) == position, IMG_DEV, counts)
    return counts.astype(jnp.int32)


def block_levels(own_key, dims, cuts, low, largest):
    factor_of, own = 1.0, jax.random.fold_in(own_key, 6)
    for dim, blocks in cuts:
        heights = jnp.exp(jax.random.uniform(jax.random.fold_in(own, dim), (blocks,), jnp.float32, low / len(cuts), largest / len(cuts)))
        factor_of = factor_of * jnp.repeat(heights, dims[dim] // blocks).reshape([-1 if axis == dim else 1 for axis in range(len(dims))])
    return factor_of


def scatter_about(key, extent, width, reach, cuts=(), held_as=jnp.bfloat16):
    factor_of = block_levels(key, extent, cuts, -0.22, 0.18) if cuts else 1.0
    values = jax.random.normal(key, extent, jnp.float32) * width * factor_of
    return jnp.minimum(jnp.maximum(values, -reach), reach).astype(held_as)


def setup_inputs(seed: int = 0) -> dict:
    arg_keys = jax.random.split(jax.random.key(seed), 12)
    images_in = scatter_about(arg_keys[0], (IMAGES, SIDE * SIDE, D), 1.0, 6.0, ((0, 32),))
    norm_gains = jnp.clip(1.0 + 0.15 * jax.random.normal(arg_keys[1], (LAYERS, 2, D), jnp.float32), 0.25, 1.75).astype(jnp.bfloat16)
    norm_biases = scatter_about(arg_keys[2], (LAYERS, 2, D), 0.3, 3.0, ((2, 16),))
    qkv_weight = scatter_about(arg_keys[3], (LAYERS, D, 3 * D), (D // 2) ** -0.5, 0.375, ((1, 16),))
    proj_weight = scatter_about(arg_keys[4], (LAYERS, D, D), (D // 8) ** -0.5, 0.75, ((1, 16),))
    up_weight = scatter_about(arg_keys[5], (LAYERS, D, FF), D ** -0.5, 0.25, ((1, 16),))
    up_bias = scatter_about(arg_keys[6], (LAYERS, FF), 0.5, 3.0, ((1, 16),))
    down_weight = scatter_about(arg_keys[7], (LAYERS, FF, D), (FF // 4) ** -0.5, 0.25, ((1, 16),))
    rel_table = scatter_about(arg_keys[8], (LAYERS, REL, HEADS), 0.5, 3.0, (), jnp.float32)
    image_counts = draw_image_counts(jax.random.fold_in(arg_keys[11], 71), 0)
    cotangent = scatter_about(arg_keys[10], (IMAGES, SIDE * SIDE, D), 1.0, 6.0, ((0, 32),))
    return {"images_in": images_in, "norm_gains": norm_gains, "norm_biases": norm_biases, "qkv_weight": qkv_weight, "proj_weight": proj_weight, "up_weight": up_weight, "up_bias": up_bias, "down_weight": down_weight, "rel_table": rel_table, "image_counts": image_counts, "cotangent": cotangent}


@jax.custom_vjp
def low(v):
    return lax.optimization_barrier(v.astype(jnp.bfloat16)).astype(jnp.float32)

@jax.custom_vjp
def low_back(v):
    return v

def low_keep(v):
    return (low(v), None)

def low_pass(kept, grad):
    return (grad,)

def back_keep(v):
    return (v, None)

def back_low(kept, grad):
    return (low(grad),)
low.defvjp(low_keep, low_pass)
low_back.defvjp(back_keep, back_low)
HIGHEST = lax.Precision.HIGHEST
EPSILON = 1e-05

def rel_onehot():
    cell_ids = jnp.arange(WIN * WIN)
    rows_of = cell_ids // WIN
    cols_of = cell_ids % WIN
    rel_index = (rows_of[:, None] - rows_of[None, :] + WIN - 1) * (2 * WIN - 1) + (cols_of[:, None] - cols_of[None, :] + WIN - 1)
    return (rel_index.reshape(-1)[:, None] == jnp.arange((2 * WIN - 1) ** 2)[None, :]).astype(jnp.float32)

def region_mask(shift_by):
    per_side = SIDE // WIN
    if shift_by == 0:
        return jnp.zeros((per_side * per_side, WIN * WIN, WIN * WIN), jnp.float32)
    positions = jnp.arange(SIDE)
    band_of = jnp.where(positions < SIDE - WIN, 0, jnp.where(positions < SIDE - shift_by, 1, 2))
    region = band_of[:, None] * 3 + band_of[None, :]
    region = region.reshape(per_side, WIN, per_side, WIN).transpose(0, 2, 1, 3).reshape(per_side * per_side, WIN * WIN)
    return jnp.where(region[:, :, None] != region[:, None, :], -100.0, 0.0).astype(jnp.float32)

def window_split(inputs, shift_by):
    images = inputs.shape[0]
    per_side = SIDE // WIN
    grid_view = inputs.reshape(images, SIDE, SIDE, -1)
    grid_view = jnp.roll(grid_view, (-shift_by, -shift_by), axis=(1, 2))
    grid_view = grid_view.reshape(images, per_side, WIN, per_side, WIN, -1).transpose(0, 1, 3, 2, 4, 5)
    return grid_view.reshape(images * per_side * per_side, WIN * WIN, -1)

def window_merge(windows, shift_by):
    per_side = SIDE // WIN
    images = windows.shape[0] // (per_side * per_side)
    grid_view = windows.reshape(images, per_side, per_side, WIN, WIN, -1).transpose(0, 1, 3, 2, 4, 5)
    grid_view = grid_view.reshape(images, SIDE, SIDE, -1)
    grid_view = jnp.roll(grid_view, (shift_by, shift_by), axis=(1, 2))
    return grid_view.reshape(images, SIDE * SIDE, -1)

def layer_norm(inputs, gain_vec, offset_vec):
    center = lax.optimization_barrier(jnp.mean(inputs, -1, keepdims=True))
    spread = lax.optimization_barrier(jnp.mean(jnp.square(inputs - center), -1, keepdims=True))
    return (inputs - center) * lax.rsqrt(spread + EPSILON) * gain_vec + offset_vec

def score_terms(queries, key_rows, pos_bias, region_add):
    scores = jnp.einsum('wihd,wjhd->whij', queries, key_rows, precision=HIGHEST)
    shape_all = scores.shape
    per_image = region_add.shape[0]
    grouped = scores.reshape(shape_all[0] // per_image, per_image, shape_all[1], shape_all[2], shape_all[3])
    grouped = grouped + pos_bias[None, None] + region_add[None, :, None]
    return grouped.reshape(shape_all)

def layer_apply(current, params, shift_by, onehot):
    norm_gain, norm_offset, w_qkv, w_proj, w_up, bias_up, w_down, table = params
    head_count = table.shape[1]
    head_size = D // head_count
    q_scale = head_size ** (-0.5)
    cell_count = WIN * WIN
    pos_bias = jnp.dot(onehot, table, precision=HIGHEST).reshape(cell_count, cell_count, head_count).transpose(2, 0, 1)
    region_add = region_mask(shift_by)
    windows = low(window_split(layer_norm(current, norm_gain[0], norm_offset[0]), shift_by))
    window_count = windows.shape[0]
    projected = low_back(jnp.dot(windows, w_qkv, precision=HIGHEST))
    queries = low(projected[:, :, :D] * q_scale).reshape(window_count, cell_count, head_count, head_size)
    key_rows = low(projected[:, :, D:2 * D]).reshape(window_count, cell_count, head_count, head_size)
    values = low(projected[:, :, 2 * D:]).reshape(window_count, cell_count, head_count, head_size)
    scores = low_back(score_terms(queries, key_rows, pos_bias, region_add))
    row_max = lax.optimization_barrier(jnp.max(scores, -1, keepdims=True))
    exponent = jnp.exp(scores - row_max)
    attn_prob = exponent / lax.optimization_barrier(jnp.sum(exponent, -1, keepdims=True))
    attended = jnp.einsum('whij,wjhd->wihd', low(attn_prob), values, precision=HIGHEST).reshape(window_count, cell_count, D)
    attended = low(low_back(attended))
    branch = low_back(jnp.dot(attended, w_proj, precision=HIGHEST))
    middle = current + window_merge(branch, shift_by)
    normed = low(layer_norm(middle, norm_gain[1], norm_offset[1]))
    hidden = low_back(jnp.dot(normed, w_up, precision=HIGHEST) + bias_up)
    active = low(jax.nn.gelu(hidden, approximate=False))
    return middle + low_back(jnp.dot(active, w_down, precision=HIGHEST))

def reference(images_in, norm_gains, norm_biases, qkv_weight, proj_weight, up_weight, up_bias, down_weight, rel_table, image_counts, cotangent):
    params = tuple((argument.astype(jnp.float32) for argument in (norm_gains, norm_biases, qkv_weight, proj_weight, up_weight, up_bias, down_weight, rel_table)))
    onehot = rel_onehot()
    image_total = images_in.shape[0]
    slot_index = jnp.arange(image_total, dtype=jnp.int32)
    valid_mask = (slot_index % IMG_DEV < jnp.repeat(image_counts, IMG_DEV)).astype(jnp.float32)
    seed_grads = cotangent.astype(jnp.float32) * valid_mask[:, None, None]
    group_size = 16
    inputs = images_in.astype(jnp.float32).reshape(image_total // group_size, group_size, SIDE * SIDE, D)
    seed_grads = seed_grads.reshape(image_total // group_size, group_size, SIDE * SIDE, D)

    def forward(weights, current):
        for level_idx in range(LAYERS):
            current = layer_apply(current, tuple((member[level_idx] for member in weights)), SHIFT * (level_idx % 2), onehot)
        return current

    def scan_step(totals, pieces):
        current, seed_now = pieces
        result, pullback = jax.vjp(forward, params, current)
        grad_params, grad_current = pullback(seed_now)
        totals = jax.tree.map(jnp.add, totals, grad_params)
        return (totals, (result, grad_current))
    zero_grads = jax.tree.map(jnp.zeros_like, params)
    totals, outputs = lax.scan(scan_step, zero_grads, (inputs, seed_grads))
    results, grad_fields = outputs
    return (results.reshape(image_total, SIDE * SIDE, D), grad_fields.reshape(image_total, SIDE * SIDE, D), totals[0], totals[1], totals[2], totals[3], totals[4], totals[5], totals[6], totals[7])
```

```python
from functools import partial

import jax
import jax.numpy as jnp
import numpy as np
from jax import lax
from jax.experimental import pallas as pl
from jax.experimental.pallas import tpu as pltpu
from jax.sharding import PartitionSpec as P

WIN = 7
SIDE = 14
SHIFT = 3
LAYERS = 2
CELLS = WIN * WIN
TOKENS = SIDE * SIDE
WROWS = 64
TROWS = 208
IROWS = 256
PACK = 4
STEP_IMAGES = 2
EPSILON = 1e-05
MASKED = -1e30
BF = jnp.bfloat16
F32 = jnp.float32


def token_order(shift_by):
    cells = np.arange(TOKENS).reshape(SIDE, SIDE)
    cells = np.roll(cells, (-shift_by, -shift_by), axis=(0, 1))
    per_side = SIDE // WIN
    return (
        cells.reshape(per_side, WIN, per_side, WIN).transpose(0, 2, 1, 3).reshape(-1, CELLS)
    )


def permutation(shift_by):
    order = token_order(shift_by)
    matrix = np.zeros((IROWS, TROWS), np.float32)
    for window in range(order.shape[0]):
        matrix[window * WROWS + np.arange(CELLS), order[window]] = 1.0
    return matrix


def region_table(shift_by):
    per_side = SIDE // WIN
    windows = per_side * per_side
    table = np.zeros((windows, WROWS, WROWS), np.float32)
    if shift_by:
        positions = np.arange(SIDE)
        band = np.where(positions < SIDE - WIN, 0, np.where(positions < SIDE - shift_by, 1, 2))
        region = band[:, None] * 3 + band[None, :]
        region = (
            region.reshape(per_side, WIN, per_side, WIN).transpose(0, 2, 1, 3).reshape(windows, -1)
        )
        table[:, :CELLS, :CELLS] = np.where(
            region[:, :, None] != region[:, None, :], -100.0, 0.0
        )
    table[:, :, CELLS:] = MASKED
    return table


def rel_selector():
    cell = np.arange(CELLS)
    rows, cols = cell // WIN, cell % WIN
    index = (rows[:, None] - rows[None, :] + WIN - 1) * (2 * WIN - 1) + (
        cols[:, None] - cols[None, :] + WIN - 1
    )
    full = np.full((WROWS, WROWS), -1)
    full[:CELLS, :CELLS] = index
    return full


def head_mask(head_size):
    lanes = np.arange(PACK * head_size) // head_size
    return np.repeat((lanes[None, :] == np.arange(PACK)[:, None]).astype(np.float32), WROWS, axis=0)


def segment_ones():
    seg = np.arange(PACK * WROWS) // WROWS
    return (seg[:, None] == seg[None, :]).astype(np.float32)


def mm(a, b):
    return lax.dot_general(a, b, (((1,), (0,)), ((), ())), preferred_element_type=F32)


def mm_nt(a, b):
    return lax.dot_general(a, b, (((1,), (1,)), ((), ())), preferred_element_type=F32)


def mm_tn(a, b):
    return lax.dot_general(a, b, (((0,), (0,)), ((), ())), preferred_element_type=F32)


def norm_parts(v):
    center = jnp.mean(v, -1, keepdims=True)
    diff = v - center
    rstd = lax.rsqrt(jnp.mean(diff * diff, -1, keepdims=True) + EPSILON)
    return diff * rstd, rstd


def norm_back(err, v, gain):
    xhat, rstd = norm_parts(v)
    scaled = err * gain
    grad = rstd * (
        scaled
        - jnp.mean(scaled, -1, keepdims=True)
        - xhat * jnp.mean(scaled * xhat, -1, keepdims=True)
    )
    return grad, jnp.sum(err * xhat, 0, keepdims=True), jnp.sum(err, 0, keepdims=True)


def pad_images(ref, buf):
    for i in range(STEP_IMAGES):
        base = i * TROWS
        buf[base + TOKENS // 8 * 8 : base + TROWS] = jnp.zeros(
            (TROWS - TOKENS // 8 * 8, buf.shape[1]), F32
        )
        buf[base : base + TOKENS] = ref[i].astype(F32)
    return buf[...]


def unpad_images(value, ref):
    for i in range(STEP_IMAGES):
        ref[i] = value[i * TROWS : i * TROWS + TOKENS]


def to_windows(perm, low):
    return [
        mm(perm, low[i * TROWS : (i + 1) * TROWS]).astype(BF) for i in range(STEP_IMAGES)
    ]


def from_windows(perm_t, low):
    return jnp.concatenate(
        [mm(perm_t, low[i * IROWS : (i + 1) * IROWS]) for i in range(STEP_IMAGES)], 0
    )


def slabs(ref, rows, start, size):
    first = start // rows
    return jnp.concatenate([ref[first + k, :rows] for k in range(size // rows)], 0)


def forward_kernel(
    first, last, masked, slab_rows, x_ref, perm_ref, perm_t_ref, hmask_ref, ones_ref, bias_ref,
    qkv_w, proj_w, up_w, down_w, gain_ref, offset_ref, up_b,
    h1_ref, qkv_ref, prob_ref, att_ref, middle_ref, h2_ref, active_ref, dgelu_ref, out_ref, buf,
):
    width = proj_w.shape[0]
    x = pad_images(x_ref, buf) if first else x_ref[...]
    gains, offsets = gain_ref[...], offset_ref[...]
    h1 = (norm_parts(x)[0] * gains[0:1] + offsets[0:1]).astype(BF)
    h1w = jnp.concatenate(to_windows(perm_ref[...], h1), 0)
    h1_ref[...] = h1w
    quad = hmask_ref.shape[1]
    head_size = quad // PACK
    for part in range(3):
        cols = slice(part * width, (part + 1) * width)
        mixed = mm(h1w, qkv_w[:, cols])
        if part == 0:
            mixed = mixed * head_size ** (-0.5)
        qkv_ref[:, cols] = mixed.astype(BF)
    hmask = hmask_ref[...]
    ones = ones_ref[...]
    lane = lax.broadcasted_iota(jnp.int32, (WROWS, 2 * WROWS), 1) < WROWS

    def window(idx, carry):
        rows = pl.ds(pl.multiple_of(idx * WROWS, WROWS), WROWS)
        place = lax.rem(idx, 4) if masked else 0
        for c in range(width // quad):
            cols = slice(c * quad, (c + 1) * quad)
            q = qkv_ref[rows, cols]
            k = qkv_ref[rows, width + c * quad : width + (c + 1) * quad]
            v = qkv_ref[rows, 2 * width + c * quad : 2 * width + (c + 1) * quad]
            k_all = jnp.concatenate([k] * PACK, 0) * hmask
            v_all = jnp.concatenate([v] * PACK, 0) * hmask
            s = mm_nt(q, k_all) + bias_ref[place, c]
            tops = []
            for half in range(PACK // 2):
                piece = s[:, half * 2 * WROWS : (half + 1) * 2 * WROWS]
                low = jnp.max(jnp.where(lane, piece, -jnp.inf), -1, keepdims=True)
                high = jnp.max(jnp.where(lane, -jnp.inf, piece), -1, keepdims=True)
                tops.append(jnp.where(lane, low, high))
            e = jnp.exp(s - jnp.concatenate(tops, 1))
            total = mm(e.astype(BF), ones)
            prob = (e / total).astype(BF)
            prob_ref[rows, c * PACK * WROWS : (c + 1) * PACK * WROWS] = prob
            att_ref[rows, cols] = mm(prob, v_all).astype(BF)
        return carry

    lax.fori_loop(0, STEP_IMAGES * 4, window, 0)
    att = from_windows(perm_t_ref[...], att_ref[...]).astype(BF)
    middle = x + mm(att, proj_w[...])
    middle_ref[...] = middle
    h2 = (norm_parts(middle)[0] * gains[1:2] + offsets[1:2]).astype(BF)
    h2_ref[...] = h2
    out = middle
    chunk = width
    for c in range(up_w.shape[1] // chunk):
        cols = slice(c * chunk, (c + 1) * chunk)
        hidden = mm(h2, up_w[:, cols]) + up_b[:, cols]
        cdf = 0.5 + 0.5 * lax.erf(hidden * (0.5**0.5))
        pdf = jnp.exp(hidden * hidden * -0.5) * ((2.0 * np.pi) ** -0.5)
        active = (hidden * cdf).astype(BF)
        active_ref[:, cols] = active
        dgelu_ref[:, cols] = (cdf + hidden * pdf).astype(BF)
        out = out + mm(active, slabs(down_w, slab_rows, c * chunk, chunk))
    if last:
        unpad_images(out, out_ref)
    else:
        out_ref[...] = out


def mlp_back_kernel(
    last, slab_rows, *refs
):
    if last:
        (count_ref, g_ref, middle_ref, dgelu_ref, up_w, down_w, gain_ref,
         low_ref, dh_ref, gmid_ref, norm_ref, ub_ref, buf) = refs
    else:
        (g_ref, middle_ref, dgelu_ref, up_w, down_w, gain_ref,
         low_ref, dh_ref, gmid_ref, norm_ref, ub_ref) = refs
    step = pl.program_id(0)
    width = up_w.shape[0]
    if last:
        for i in range(STEP_IMAGES):
            base = i * TROWS
            buf[base + TOKENS // 8 * 8 : base + TROWS] = jnp.zeros(
                (TROWS - TOKENS // 8 * 8, width), F32
            )
            keep = jnp.where(step * STEP_IMAGES + i < count_ref[0], 1.0, 0.0).astype(F32)
            buf[base : base + TOKENS] = g_ref[i].astype(F32) * keep
        g = buf[...]
    else:
        g = g_ref[...]
    low = g.astype(BF)
    low_ref[...] = low
    d_h2 = jnp.zeros(g.shape, F32)
    chunk = width
    sums = []
    for c in range(up_w.shape[1] // chunk):
        cols = slice(c * chunk, (c + 1) * chunk)
        d_active = mm_nt(low, slabs(down_w, slab_rows, c * chunk, chunk))
        dh = d_active * dgelu_ref[:, cols].astype(F32)
        sums.append(jnp.sum(dh, 0, keepdims=True))
        dh = dh.astype(BF)
        dh_ref[:, cols] = dh
        d_h2 = d_h2 + mm_nt(dh, up_w[:, cols])
    back, d_gain, d_offset = norm_back(d_h2, middle_ref[...], gain_ref[1:2])
    gmid_ref[...] = g + back
    parts = jnp.concatenate([d_gain, d_offset], 0)
    ub = jnp.concatenate(sums, 1)

    @pl.when(step == 0)
    def _():
        norm_ref[...] = parts
        ub_ref[...] = ub

    @pl.when(step > 0)
    def _():
        norm_ref[...] += parts
        ub_ref[...] += ub


def attention_back_kernel(
    first, gmid_ref, x_ref, qkv_ref, prob_ref, att_ref, perm_ref, perm_t_ref, hmask_ref, spread_ref,
    proj_w, qkv_w, gain_ref,
    branch_ref, mixed_ref, out_ref, ssum_ref, norm_ref, datt_ref, *extra
):
    step = pl.program_id(0)
    width = proj_w.shape[0]
    g_mid = gmid_ref[...]
    branch = jnp.concatenate(to_windows(perm_ref[...], g_mid.astype(BF)), 0)
    branch_ref[...] = branch
    datt_ref[...] = mm_nt(branch, proj_w[...]).astype(BF)
    hmask = hmask_ref[...]
    spread = spread_ref[...]
    quad = hmask.shape[1]
    head_size = quad // PACK
    lane_head = lax.broadcasted_iota(jnp.int32, (WROWS, quad), 1) // head_size

    @pl.when(step == 0)
    def _():
        ssum_ref[...] = jnp.zeros(ssum_ref.shape, F32)

    def fold(stacked):
        out = stacked[:WROWS]
        for h in range(1, PACK):
            out = jnp.where(lane_head == h, stacked[h * WROWS : (h + 1) * WROWS], out)
        return out

    def window(idx, carry):
        rows = pl.ds(pl.multiple_of(idx * WROWS, WROWS), WROWS)
        for c in range(width // quad):
            cols = slice(c * quad, (c + 1) * quad)
            k_cols = slice(width + c * quad, width + (c + 1) * quad)
            v_cols = slice(2 * width + c * quad, 2 * width + (c + 1) * quad)
            q = qkv_ref[rows, cols]
            k_all = jnp.concatenate([qkv_ref[rows, k_cols]] * PACK, 0) * hmask
            v_all = jnp.concatenate([qkv_ref[rows, v_cols]] * PACK, 0) * hmask
            d_o = datt_ref[rows, cols]
            prob = prob_ref[rows, c * PACK * WROWS : (c + 1) * PACK * WROWS]
            d_prob = mm_nt(d_o, v_all)
            both = d_o.astype(F32) * att_ref[rows, cols].astype(F32)
            coarse = both.astype(BF)
            fine = (both - coarse.astype(F32)).astype(BF)
            center = mm(jnp.concatenate([coarse, fine], 1), spread)
            d_s = (prob.astype(F32) * (d_prob - center)).astype(BF)
            ssum_ref[c] += d_s.astype(F32)
            d_q = mm(d_s, k_all) * head_size ** (-0.5)
            d_k = fold(mm_tn(d_s, q))
            d_v = fold(mm_tn(prob, d_o))
            mixed_ref[rows, cols] = d_q.astype(BF)
            mixed_ref[rows, k_cols] = d_k.astype(BF)
            mixed_ref[rows, v_cols] = d_v.astype(BF)
        return carry

    lax.fori_loop(0, STEP_IMAGES * 4, window, 0)
    d_h1w = mm_nt(mixed_ref[...], qkv_w[...]).astype(BF)
    d_h1 = from_windows(perm_t_ref[...], d_h1w)
    x = pad_images(x_ref, extra[0]) if first else x_ref[...]
    back, d_gain, d_offset = norm_back(d_h1, x, gain_ref[0:1])
    out = g_mid + back
    if first:
        unpad_images(out, out_ref)
    else:
        out_ref[...] = out
    parts = jnp.concatenate([d_gain, d_offset], 0)

    @pl.when(step == 0)
    def _():
        norm_ref[...] = parts

    @pl.when(step > 0)
    def _():
        norm_ref[...] += parts


def rows_spec(rows, cols):
    return pl.BlockSpec((rows, cols), lambda i: (i, 0))


def image_spec(cols):
    return pl.BlockSpec((STEP_IMAGES, TOKENS, cols), lambda i: (i, 0, 0))


def whole(array):
    zeros = (0,) * array.ndim
    return pl.BlockSpec(array.shape, lambda i: zeros)


def constants(shift_by, head_size):
    perm = permutation(shift_by)
    hmask = head_mask(head_size)
    spread = np.concatenate([hmask.T, hmask.T], 0)
    return dict(
        perm=jnp.asarray(perm, BF),
        perm_t=jnp.asarray(perm.T, BF),
        hmask=jnp.asarray(hmask, BF),
        ones=jnp.asarray(segment_ones(), BF),
        spread=jnp.asarray(spread, BF),
    )


def out_rows(rows, cols, dtype):
    return jax.ShapeDtypeStruct((rows, cols), dtype)


VMEM_LIMIT = 60 * 1024 * 1024


def params():
    return pltpu.CompilerParams(
        vmem_limit_bytes=VMEM_LIMIT, dimension_semantics=("arbitrary",)
    )


def block_forward(x, consts, bias, weights, first, last, slab_rows):
    qkv_w, proj_w, up_w, down_w, gains, offsets, up_b = weights
    width, ff = up_w.shape
    heads = bias.shape[1] * PACK
    images = x.shape[0] if first else x.shape[0] // TROWS
    rows, wrows = images * TROWS, images * IROWS
    sr, sw = STEP_IMAGES * TROWS, STEP_IMAGES * IROWS
    x_spec = image_spec(width) if first else rows_spec(sr, width)
    if last:
        out_shape, out_spec = jax.ShapeDtypeStruct((images, TOKENS, width), F32), image_spec(width)
    else:
        out_shape, out_spec = out_rows(rows, width, F32), rows_spec(sr, width)
    fixed = [consts["perm"], consts["perm_t"], consts["hmask"], consts["ones"], bias, qkv_w, proj_w,
             up_w, down_w, gains, offsets, up_b]
    return pl.pallas_call(
        partial(forward_kernel, first, last, bias.shape[0] > 1, slab_rows),
        grid=(images // STEP_IMAGES,),
        in_specs=[x_spec] + [whole(a) for a in fixed],
        out_specs=[
            rows_spec(sw, width), rows_spec(sw, 3 * width), rows_spec(sw, heads * WROWS),
            rows_spec(sw, width), rows_spec(sr, width), rows_spec(sr, width), rows_spec(sr, ff),
            rows_spec(sr, ff), out_spec,
        ],
        out_shape=[
            out_rows(wrows, width, BF), out_rows(wrows, 3 * width, BF),
            out_rows(wrows, heads * WROWS, BF), out_rows(wrows, width, BF),
            out_rows(rows, width, F32), out_rows(rows, width, BF), out_rows(rows, ff, BF),
            out_rows(rows, ff, BF), out_shape,
        ],
        scratch_shapes=[pltpu.VMEM((sr, width), F32)],
        compiler_params=params(),
        cost_estimate=pl.CostEstimate(
            flops=2 * rows * width * (4 * width + 2 * ff) * 2, bytes_accessed=40_000_000,
            transcendentals=rows * ff,
        ),
        name="block_forward",
    )(x, *fixed)


def mlp_backward(grad, count, middle, dgelu, weights, last, slab_rows):
    up_w, down_w, gains = weights
    width, ff = up_w.shape
    rows = middle.shape[0]
    sr = STEP_IMAGES * TROWS
    tensors = [grad, middle, dgelu]
    specs = [image_spec(width) if last else rows_spec(sr, width), rows_spec(sr, width), rows_spec(sr, ff)]
    if last:
        tensors = [count] + tensors
        specs = [pl.BlockSpec(memory_space=pltpu.SMEM)] + specs
    fixed = [up_w, down_w, gains]
    return pl.pallas_call(
        partial(mlp_back_kernel, last, slab_rows),
        grid=(rows // sr,),
        in_specs=specs + [whole(a) for a in fixed],
        out_specs=[
            rows_spec(sr, width), rows_spec(sr, ff), rows_spec(sr, width),
            pl.BlockSpec((2, width), lambda i: (0, 0)), pl.BlockSpec((1, ff), lambda i: (0, 0)),
        ],
        out_shape=[
            out_rows(rows, width, BF), out_rows(rows, ff, BF), out_rows(rows, width, F32),
            out_rows(2, width, F32), out_rows(1, ff, F32),
        ],
        scratch_shapes=[pltpu.VMEM((sr, width), F32)] if last else [],
        compiler_params=params(),
        cost_estimate=pl.CostEstimate(
            flops=2 * rows * width * 2 * ff, bytes_accessed=25_000_000, transcendentals=0
        ),
        name="mlp_backward",
    )(*tensors, *fixed)


def attention_backward(g_mid, x, saved, consts, weights, first):
    qkv, prob, att = saved
    proj_w, qkv_w, gains = weights
    width = proj_w.shape[0]
    rows = g_mid.shape[0]
    images = rows // TROWS
    wrows = images * IROWS
    sr, sw = STEP_IMAGES * TROWS, STEP_IMAGES * IROWS
    quads = prob.shape[1] // (PACK * WROWS)
    if first:
        out_shape, out_spec = jax.ShapeDtypeStruct((images, TOKENS, width), F32), image_spec(width)
    else:
        out_shape, out_spec = out_rows(rows, width, F32), rows_spec(sr, width)
    fixed = [consts["perm"], consts["perm_t"], consts["hmask"], consts["spread"], proj_w, qkv_w, gains]
    scratch = [pltpu.VMEM((sw, width), BF)]
    if first:
        scratch.append(pltpu.VMEM((sr, width), F32))
    return pl.pallas_call(
        partial(attention_back_kernel, first),
        grid=(images // STEP_IMAGES,),
        in_specs=[
            rows_spec(sr, width), image_spec(width) if first else rows_spec(sr, width),
            rows_spec(sw, 3 * width), rows_spec(sw, prob.shape[1]), rows_spec(sw, width),
        ] + [whole(a) for a in fixed],
        out_specs=[
            rows_spec(sw, width), rows_spec(sw, 3 * width), out_spec,
            pl.BlockSpec((quads, WROWS, PACK * WROWS), lambda i: (0, 0, 0)),
            pl.BlockSpec((2, width), lambda i: (0, 0)),
        ],
        out_shape=[
            out_rows(wrows, width, BF), out_rows(wrows, 3 * width, BF), out_shape,
            jax.ShapeDtypeStruct((quads, WROWS, PACK * WROWS), F32), out_rows(2, width, F32),
        ],
        scratch_shapes=scratch,
        compiler_params=params(),
        cost_estimate=pl.CostEstimate(
            flops=2 * rows * width * 8 * width, bytes_accessed=35_000_000, transcendentals=0
        ),
        name="attention_backward",
    )(g_mid, x, qkv, prob, att, *fixed)


def weight_grad(left, right):
    return lax.dot_general(
        left, right, (((0,), (0,)), ((), ())), preferred_element_type=F32
    ).astype(BF)


def body(
    images_in, norm_gains, norm_biases, qkv_weight, proj_weight, up_weight, up_bias, down_weight,
    rel_table, image_counts, cotangent,
):
    width = images_in.shape[-1]
    heads = rel_table.shape[-1]
    head_size = width // heads
    quads = heads // PACK
    group = lax.axis_size("shard")
    part = width // group
    ff_part = down_weight.shape[1]
    ff = ff_part * group
    slab_rows = ff_part

    small = jnp.concatenate(
        [norm_gains.reshape(-1), norm_biases.reshape(-1), up_bias.reshape(-1)]
    )
    small_size = small.shape[0]
    extra = -(-small_size // (16 * width)) * 16
    small_rows = jnp.pad(small, (0, extra * width - small_size)).reshape(extra, width)
    gathered = []
    for l in range(LAYERS):
        down = down_weight[l]
        if l == 0:
            down = jnp.concatenate([down, small_rows], 0)
        row_block = jnp.concatenate([qkv_weight[l], proj_weight[l], up_weight[l]], 1)
        rows_all = lax.all_gather(row_block, "shard", axis=0, tiled=True)
        down_all = lax.all_gather(down, "shard", axis=0, tiled=False)
        gathered.append((rows_all, down_all))
    small_all = gathered[0][1][:, ff_part:].reshape(group, -1)[:, :small_size].astype(F32)
    n_norm = LAYERS * 2 * part
    gains = small_all[:, :n_norm].reshape(group, LAYERS, 2, part)
    gains = gains.transpose(1, 2, 0, 3).reshape(LAYERS, 2, width)
    offsets = small_all[:, n_norm : 2 * n_norm].reshape(group, LAYERS, 2, part)
    offsets = offsets.transpose(1, 2, 0, 3).reshape(LAYERS, 2, width)
    up_b = small_all[:, 2 * n_norm :].reshape(group, LAYERS, ff_part)
    up_b = up_b.transpose(1, 0, 2).reshape(LAYERS, ff)

    selector = rel_selector()
    rel_count = rel_table.shape[1]
    onehot = jnp.asarray(
        (selector.reshape(-1)[None, :] == np.arange(rel_count)[:, None]).astype(np.float32), BF
    )
    pos = lax.dot_general(
        rel_table, onehot.astype(F32), (((1,), (0,)), ((), ())), precision=lax.Precision.HIGHEST
    )
    pos = pos.reshape(LAYERS, quads, PACK, WROWS, WROWS).transpose(0, 1, 3, 2, 4)
    pos = pos.reshape(LAYERS, quads, WROWS, PACK * WROWS)

    x = images_in
    kept = []
    for l in range(LAYERS):
        shift_by = SHIFT * (l % 2)
        consts = constants(shift_by, head_size)
        region = region_table(shift_by)
        if not shift_by:
            region = region[:1]
        region = jnp.asarray(np.tile(region, (1, 1, PACK)), F32)
        bias = pos[l][None] + region[:, None]
        rows_all, down_all = gathered[l]
        qkv_w, proj_w, up_w = (
            rows_all[:, : 3 * width], rows_all[:, 3 * width : 4 * width], rows_all[:, 4 * width :]
        )
        weights = (qkv_w, proj_w, up_w, down_all, gains[l], offsets[l], up_b[l][None])
        outs = block_forward(x, consts, bias, weights, l == 0, l == LAYERS - 1, slab_rows)
        kept.append((x, outs, weights, consts))
        x = outs[-1]
    block_out = x

    grad = cotangent
    big = [None] * LAYERS
    norm_grads = [None] * LAYERS
    up_grads = [None] * LAYERS
    score_sums = [None] * LAYERS

    def scatter(value):
        return lax.psum_scatter(value, "shard", scatter_dimension=0, tiled=True)

    for l in reversed(range(LAYERS)):
        x, outs, weights, consts = kept[l]
        h1w, qkv, prob, att, middle, h2, active, dgelu, _ = outs
        qkv_w, proj_w, up_w, down_all, gain, _, _ = weights
        low, d_hidden, g_mid, norm_two, up_sum = mlp_backward(
            grad, image_counts, middle, dgelu, (up_w, down_all, gain), l == LAYERS - 1, slab_rows
        )
        g_down = scatter(weight_grad(active, low))
        g_up = scatter(weight_grad(h2, d_hidden))
        d_branch, d_mixed, grad, ssum, norm_one = attention_backward(
            g_mid, x, (qkv, prob, att), consts, (proj_w, qkv_w, gain), l == 0
        )
        g_proj = scatter(weight_grad(att, d_branch))
        g_qkv = scatter(weight_grad(h1w, d_mixed))
        big[l] = (g_qkv, g_proj, g_up, g_down)
        norm_grads[l] = (norm_one, norm_two)
        up_grads[l] = up_sum[0]
        score_sums[l] = ssum

    sums = jnp.stack(score_sums).reshape(LAYERS, quads, WROWS, PACK, WROWS)
    sums = sums.transpose(0, 1, 3, 2, 4).reshape(LAYERS * heads, WROWS * WROWS)
    table = lax.dot_general(
        onehot.astype(F32), sums, (((1,), (1,)), ((), ())), precision=lax.Precision.HIGHEST
    )
    table = table.reshape(rel_count, LAYERS, heads).transpose(1, 0, 2)
    norms = jnp.stack([jnp.stack(pair) for pair in norm_grads])
    ups = jnp.stack(up_grads)
    packed = jnp.concatenate([norms.reshape(-1), ups.reshape(-1), table.reshape(-1)])
    packed = lax.psum(packed, ("shard", "rep"))
    norms = packed[: norms.size].reshape(norms.shape)
    ups_all = packed[norms.size : norms.size + ups.size].reshape(ups.shape)
    table_total = packed[norms.size + ups.size :].reshape(table.shape)
    me = lax.axis_index("shard")
    norms = lax.dynamic_slice_in_dim(norms, me * part, part, 3)
    g_up_bias = lax.dynamic_slice_in_dim(ups_all, me * ff_part, ff_part, 1)
    g_gains, g_biases = norms[:, :, 0], norms[:, :, 1]

    shapes = [[g.shape for g in big[l]] for l in range(LAYERS)]
    summed = lax.psum(tuple(g for l in range(LAYERS) for g in big[l]), "rep")
    count = len(big[0])
    final = [
        jnp.stack([summed[l * count + m].astype(F32) for l in range(LAYERS)]) for m in range(count)
    ]
    g_qkv, g_proj, g_up, g_down = final
    return (
        block_out, grad, g_gains, g_biases, g_qkv, g_proj, g_up, g_up_bias, g_down, table_total
    )


def solution(mesh):
    in_specs = (
        P(("shard", "rep"), None, None),
        P(None, None, "shard"),
        P(None, None, "shard"),
        P(None, "shard", None),
        P(None, "shard", None),
        P(None, "shard", None),
        P(None, "shard"),
        P(None, "shard", None),
        P(),
        P(("shard", "rep")),
        P(("shard", "rep"), None, None),
    )
    out_specs = (
        P(("shard", "rep"), None, None),
        P(("shard", "rep"), None, None),
        P(None, None, "shard"),
        P(None, None, "shard"),
        P(None, "shard", None),
        P(None, "shard", None),
        P(None, "shard", None),
        P(None, "shard"),
        P(None, "shard", None),
        P(),
    )
    return jax.shard_map(body, mesh=mesh, in_specs=in_specs, out_specs=out_specs, check_vma=False)
```
